32 devices in a mesh: tm: 8 (over y, x, core), group: 4 (over z).
Axes of the slice: x: 2, y: 2, z: 4, core: 2. Of those that a mesh axis runs over, the one named last changes fastest.
Arguments:
- tokens: bfloat16 [8, 1024, 1024], P('tm', 'group'), may hold values from -6 to 6
- conv_weight: float32 [3, 1024], replicated, may hold values from -3 to 3
- qkv_weight: bfloat16 [1024, 3072], replicated, may hold values from -0.1875 to 0.1875
- attn_out_weight: bfloat16 [1024, 1024], replicated, may hold values from -0.1875 to 0.1875
- router_weight: bfloat16 [1024, 16], replicated, may hold values from -0.375 to 0.375
- expert_ids: int32 [8, 1024, 2], P('tm', 'group'), may hold values from 0 to 15, as said below
- expert_in: bfloat16 [32, 1024, 2048], P(('tm', 'group')), may hold values from -0.1875 to 0.1875
- expert_out: bfloat16 [32, 2048, 1024], P(('tm', 'group')), may hold values from -0.09375 to 0.09375
Outputs:
- layer_out: bfloat16 [8, 1024, 1024], P('tm', 'group')
The draws below stay inside these ranges and needn't reach their ends.
Inputs may be any that keep to these rules, and one draw needn't show every extreme that they name: `expert_ids`: each row names two different experts. In the rows of one device (one frame, 256 consecutive spatial positions) * 4 experts are named exactly 64 times each and the others share the remaining routes as evenly as possible; one expert is among the fully named ones on every device.
All inputs are finite; a program needn't handle non-finite values.
Results may differ from the reference program's by a relative error of at most 0.0095.
Values may be sent and summed in bfloat16 or wider, within the bound.
No kernel may reach another device: no remote copies, remote signals or barrier semaphores. Data moves between devices by JAX's collectives and lax.ppermute only.
A program may use at most 128 MiB of HBM per device.

```python
import math
import jax
import jax.numpy as jnp
import numpy as np
from jax import lax

D = 1024
HEADS = 16
HD = 64
FF = 4096
SP_DEV = 256
FRAMES = 8
SPATIAL = 1024
EXPERTS = 16
FF_DEV = 2048
CAP = 64


def rank_table():
    routes = 2 * SP_DEV
    hot_count = SP_DEV // CAP
    remaining = routes - hot_count * CAP
    cold_count = EXPERTS - hot_count
    counts = np.full(EXPERTS, remaining // cold_count, dtype=np.int64)
    counts[:hot_count] = CAP
    counts[hot_count:hot_count + remaining % cold_count] += 1
    return np.repeat(np.arange(EXPERTS), counts)


def draw_expert_ids(key, part):
    blocks = FRAMES * SPATIAL // SP_DEV
    ranking = jnp.asarray(rank_table(), dtype=jnp.int32)
    favoured = jax.random.randint(jax.random.fold_in(key, 1), (), 0, EXPERTS).astype(jnp.int32)

    def one_block(block_key):
        order_key, row_key, flip_key = jax.random.split(block_key, 3)
        ordering = jax.random.permutation(order_key, EXPERTS).astype(jnp.int32)
        ordering = jnp.where(ordering == favoured, ordering[0], ordering)
        ordering = ordering.at[0].set(favoured)
        id_table = ordering[ranking].reshape(2, SP_DEV).T
        id_table = id_table[jax.random.permutation(row_key, SP_DEV)]
        flipped = jax.random.randint(flip_key, (SP_DEV, 1), 0, 2)
        return jnp.where(flipped == 1, id_table[:, ::-1], id_table)
    block_keys = jax.random.split(jax.random.fold_in(key, 2), blocks)
    tables = jax.vmap(one_block)(block_keys)
    return tables.reshape(FRAMES, SPATIAL, 2).astype(jnp.int32)


def steps_of(own_key, dims, cuts, smallest, largest):
    gain = 1.0
    for axis_at, blocks in cuts:
        steps = jax.random.uniform(jax.random.fold_in(jax.random.fold_in(own_key, 6), axis_at), (blocks,), jnp.float32, smallest / len(cuts), largest / len(cuts))
        gain = gain * jnp.repeat(jnp.exp(steps), dims[axis_at] // blocks).reshape((-1,) + (1,) * (len(dims) - 1 - axis_at))
    return gain


def gaussian(own_key, extent, width, most, shards=(), kind=jnp.bfloat16):
    drawn = jax.random.normal(own_key, extent, jnp.float32) * width
    if len(shards) > 0:
        drawn = steps_of(own_key, extent, shards, -0.22, 0.18) * drawn
    return jnp.clip(drawn, min=-most, max=most).astype(kind)


def setup_inputs(seed: int = 0) -> dict:
    seeds = jax.random.split(jax.random.key(seed), 9)
    return {
        "tokens": gaussian(seeds[0], (FRAMES, SPATIAL, D), 1.0, 6.0, ((0, 8), (1, 4))),
        "conv_weight": gaussian(seeds[1], (3, D), 0.5, 3.0, (), jnp.float32),
        "qkv_weight": gaussian(seeds[2], (D, 3 * D), D ** -0.5, 0.1875),
        "attn_out_weight": gaussian(seeds[3], (D, D), D ** -0.5, 0.1875),
        "router_weight": gaussian(seeds[4], (D, EXPERTS), (D // 4) ** -0.5, 0.375),
        "expert_ids": draw_expert_ids(jax.random.fold_in(seeds[8], 71), 0),
        "expert_in": gaussian(seeds[6], (2 * EXPERTS, D, FF_DEV), D ** -0.5, 0.1875, ((0, 32),)),
        "expert_out": gaussian(seeds[7], (2 * EXPERTS, FF_DEV, D), FF ** -0.5, 0.09375, ((0, 32),)),
    }


def layer_normed(values):
    values = values.astype(jnp.float32)
    centre = lax.optimization_barrier(jnp.mean(values, -1, keepdims=True))
    spread = lax.optimization_barrier(jnp.mean((values - centre) ** 2, -1, keepdims=True))
    return ((values - centre) / jnp.sqrt(spread + 1e-05)).astype(jnp.bfloat16)

def unit_scaled(values):
    return (values / jnp.sqrt(lax.optimization_barrier(jnp.mean(values * values, -1, keepdims=True)) + 1e-06)).astype(jnp.bfloat16)

def convolved(padded, current, conv_weight):
    summed = conv_weight[0] * padded[:-2].astype(jnp.float32) + conv_weight[1] * padded[1:-1].astype(jnp.float32) + conv_weight[2] * padded[2:].astype(jnp.float32)
    return (current.astype(jnp.float32) + summed).astype(jnp.bfloat16)

def time_mixing(normed, qkv_weight, attn_out_weight):
    frames, across, channels = normed.shape
    projected = jnp.dot(normed.reshape(frames * across, channels), qkv_weight, preferred_element_type=jnp.float32)
    projected = projected.reshape(frames, across, 3, HEADS, HD)
    queries = unit_scaled(projected[:, :, 0])
    keys_all = unit_scaled(projected[:, :, 1])
    values_all = projected[:, :, 2].astype(jnp.bfloat16)
    scores = jnp.einsum('fshd,gshd->shfg', queries.astype(jnp.float32), keys_all.astype(jnp.float32), precision=lax.Precision.HIGHEST) / math.sqrt(HD)
    weights = jnp.exp(scores)
    weights = (weights / lax.optimization_barrier(jnp.sum(weights, -1, keepdims=True))).astype(jnp.bfloat16)
    context = jnp.einsum('shfg,gshd->fshd', weights.astype(jnp.float32), values_all.astype(jnp.float32), precision=lax.Precision.HIGHEST).astype(jnp.bfloat16)
    mixed_out = jnp.dot(context.reshape(frames * across, channels), attn_out_weight, preferred_element_type=jnp.float32)
    return mixed_out.astype(jnp.bfloat16).reshape(frames, across, channels)

def half_partial(slot_rows, inner_weight, outer_weight):
    flat_rows = slot_rows.reshape(-1, slot_rows.shape[-1])
    hidden = jax.nn.gelu(jnp.dot(flat_rows, inner_weight, preferred_element_type=jnp.float32)).astype(jnp.bfloat16)
    return jnp.dot(hidden, outer_weight, preferred_element_type=jnp.float32).reshape(slot_rows.shape)

def reference(tokens, conv_weight, qkv_weight, attn_out_weight, router_weight, expert_ids, expert_in, expert_out):
    padded = jnp.pad(tokens, ((1, 1), (0, 0), (0, 0)))
    stream_one = convolved(padded, tokens, conv_weight)
    attended = time_mixing(layer_normed(stream_one), qkv_weight, attn_out_weight)
    stream_two = (stream_one.astype(jnp.float32) + attended.astype(jnp.float32)).astype(jnp.bfloat16)
    moe_rows = layer_normed(stream_two)
    blocks = FRAMES * SPATIAL // SP_DEV
    block_rows = moe_rows.reshape(blocks, SP_DEV, D)
    routed = expert_ids.reshape(blocks, SP_DEV, 2).astype(jnp.int32)
    logits = jnp.dot(moe_rows.reshape(-1, D), router_weight, preferred_element_type=jnp.float32).reshape(blocks, SP_DEV, EXPERTS)
    chosen = jnp.take_along_axis(logits, routed, axis=-1)
    gate_values = jax.nn.sigmoid(chosen)
    shares = gate_values / lax.optimization_barrier(jnp.sum(gate_values, -1, keepdims=True))
    flat_ids = routed.reshape(blocks, SP_DEV * 2)
    matches = (flat_ids[:, :, None] == jnp.arange(EXPERTS, dtype=jnp.int32)[None, None, :]).astype(jnp.int32)
    slot_index = lax.optimization_barrier(jnp.sum((jnp.cumsum(matches, 1) - matches) * matches, -1)).astype(jnp.int32)
    owners = jnp.broadcast_to(jnp.arange(blocks, dtype=jnp.int32)[:, None], flat_ids.shape)
    sources = jnp.repeat(block_rows, 2, axis=1)
    buffers = jnp.zeros((EXPERTS, blocks, CAP, D), jnp.bfloat16).at[flat_ids, owners, slot_index].set(sources)

    def serve(operands):
        buffer, inner_pair, outer_pair = operands
        first_part = half_partial(buffer, inner_pair[0], outer_pair[0])
        second_part = half_partial(buffer, inner_pair[1], outer_pair[1])
        return (first_part + second_part).astype(jnp.bfloat16)
    results = lax.map(serve, (buffers, expert_in.reshape(EXPERTS, 2, D, FF_DEV), expert_out.reshape(EXPERTS, 2, FF_DEV, D)))
    picked = results[flat_ids, owners, slot_index].reshape(blocks, SP_DEV, 2, D).astype(jnp.float32)
    moe_out = lax.optimization_barrier(jnp.sum(shares[..., None] * picked, 2))
    layer_out = stream_two.reshape(blocks, SP_DEV, D).astype(jnp.float32) + moe_out
    return layer_out.astype(jnp.bfloat16).reshape(FRAMES, SPATIAL, D)
```

```python
import math

import jax
import jax.numpy as jnp
from jax import lax
from jax.sharding import PartitionSpec as P

HD = 64


def layer_normed(values):
    values = values.astype(jnp.float32)
    centre = jnp.mean(values, -1, keepdims=True)
    spread = jnp.mean((values - centre) ** 2, -1, keepdims=True)
    return ((values - centre) / jnp.sqrt(spread + 1e-05)).astype(jnp.bfloat16)


def unit_scaled(values):
    return (values / jnp.sqrt(jnp.mean(values * values, -1, keepdims=True) + 1e-06)).astype(
        jnp.bfloat16
    )


def convolved(frames, conv_weight):
    wide = frames.astype(jnp.float32)
    padded = jnp.pad(wide, ((1, 1), (0, 0), (0, 0)))
    summed = conv_weight[0] * padded[:-2] + conv_weight[1] * wide + conv_weight[2] * padded[2:]
    return (wide + summed).astype(jnp.bfloat16)


def time_mixing(normed, qkv_weight, attn_out_weight):
    frames, across, channels = normed.shape
    heads = channels // HD
    projected = jnp.dot(
        normed.reshape(frames * across, channels), qkv_weight, preferred_element_type=jnp.float32
    )
    projected = projected.reshape(frames, across, 3, heads, HD)
    queries = unit_scaled(projected[:, :, 0])
    keys_all = unit_scaled(projected[:, :, 1])
    values_all = projected[:, :, 2].astype(jnp.bfloat16)
    scores = jnp.einsum(
        "fshd,gshd->shfg", queries, keys_all, preferred_element_type=jnp.float32
    ) / math.sqrt(HD)
    weights = jnp.exp(scores)
    weights = (weights / jnp.sum(weights, -1, keepdims=True)).astype(jnp.bfloat16)
    context = jnp.einsum(
        "shfg,gshd->fshd", weights, values_all, preferred_element_type=jnp.float32
    ).astype(jnp.bfloat16)
    mixed_out = jnp.dot(
        context.reshape(frames * across, channels),
        attn_out_weight,
        preferred_element_type=jnp.float32,
    )
    return mixed_out.astype(jnp.bfloat16).reshape(frames, across, channels)


def body(
    tokens,
    conv_weight,
    qkv_weight,
    attn_out_weight,
    router_weight,
    expert_ids,
    expert_in,
    expert_out,
):
    shards = lax.axis_size("tm")
    groups = lax.axis_size("group")
    classes = groups // 2
    mine = lax.axis_index("group") // 2
    spatial, channels = tokens.shape[1:]
    across = spatial // shards
    experts = router_weight.shape[1]
    capacity = 4 * spatial // experts

    def swapped(rows, step):
        if step == 0:
            return rows
        return lax.ppermute(rows, "group", [(i, i ^ step) for i in range(groups)])

    routed = expert_ids.reshape(spatial, 2)
    ids = [swapped(routed, step) for step in range(groups)]

    received = lax.all_to_all(
        tokens.reshape(1, shards, across, channels), "tm", split_axis=1, concat_axis=0, tiled=True
    ).reshape(shards, across, channels)
    stream_one = convolved(received, conv_weight)
    attended = time_mixing(layer_normed(stream_one), qkv_weight, attn_out_weight)
    stream_two = (stream_one.astype(jnp.float32) + attended.astype(jnp.float32)).astype(
        jnp.bfloat16
    )
    stream = lax.all_to_all(
        stream_two.reshape(shards, 1, across, channels),
        "tm",
        split_axis=0,
        concat_axis=1,
        tiled=True,
    ).reshape(spatial, channels)

    home = jnp.arange(shards, dtype=jnp.int32) * classes + mine
    blocks = [swapped(stream, step) for step in range(groups)]
    partials = []
    for step in range(groups):
        rows = layer_normed(blocks[step])
        logits = jnp.dot(rows, router_weight, preferred_element_type=jnp.float32)
        matches = ids[step][:, :, None] == jnp.arange(experts, dtype=jnp.int32)
        chosen = jnp.sum(jnp.where(matches, logits[:, None, :], 0.0), -1)
        gates = jax.nn.sigmoid(chosen)
        shares = gates / jnp.sum(gates, -1, keepdims=True)
        here = ids[step][:, :, None] == home
        weight = jnp.sum(jnp.where(here, shares[:, :, None], 0.0), 1)
        member = jnp.any(here, 1)
        order = jnp.arange(spatial, dtype=jnp.int32)
        earlier = (order[:, None] > order[None, :]).astype(jnp.bfloat16)
        rank = jnp.dot(
            earlier, member.astype(jnp.bfloat16), preferred_element_type=jnp.float32
        ).astype(jnp.int32)
        slots = jnp.arange(capacity, dtype=jnp.int32)
        picks = member[:, :, None] & (rank[:, :, None] == slots)
        send = picks.astype(jnp.bfloat16).reshape(spatial, shards * capacity)
        back = jnp.where(picks, weight[:, :, None], 0.0).astype(jnp.bfloat16)
        back = back.reshape(spatial, shards * capacity)
        outbox = lax.dot_general(
            send, rows, (((0,), (0,)), ((), ())), preferred_element_type=jnp.float32
        ).astype(jnp.bfloat16)
        inbox = lax.all_to_all(
            outbox.reshape(shards, capacity, channels), "tm", split_axis=0, concat_axis=0, tiled=True
        ).reshape(shards * capacity, channels)
        hidden = jax.nn.gelu(
            jnp.dot(inbox, expert_in[0], preferred_element_type=jnp.float32)
        ).astype(jnp.bfloat16)
        partial = jnp.dot(hidden, expert_out[0], preferred_element_type=jnp.float32)
        returned = lax.all_to_all(
            partial.astype(jnp.bfloat16).reshape(shards, capacity, channels),
            "tm",
            split_axis=0,
            concat_axis=0,
            tiled=True,
        ).reshape(shards * capacity, channels)
        mixed = jnp.dot(back, returned, preferred_element_type=jnp.float32)
        if step:
            mixed = swapped(mixed.astype(jnp.bfloat16), step).astype(jnp.float32)
        partials.append(mixed)
    total = stream.astype(jnp.float32)
    for mixed in partials:
        total = total + mixed
    return total.astype(jnp.bfloat16).reshape(1, spatial, channels)


def solution(mesh):
    placed = (
        P("tm", "group", None),
        P(),
        P(),
        P(),
        P(),
        P("tm", "group", None),
        P(("tm", "group"), None, None),
        P(("tm", "group"), None, None),
    )
    return jax.shard_map(
        body, mesh=mesh, in_specs=placed, out_specs=P("tm", "group", None), check_vma=False
    )
```

```python
import functools
import math

import jax
import jax.numpy as jnp
from jax import lax
from jax.experimental import pallas as pl
from jax.experimental.pallas import tpu as pltpu
from jax.sharding import PartitionSpec as P


HD = 64
VMEM = pl.BlockSpec(memory_space=pltpu.VMEM)
SMEM = pl.BlockSpec(memory_space=pltpu.SMEM)
LIMIT = pltpu.CompilerParams(vmem_limit_bytes=28 * 2**20)


def layer_normed(values):
    values = values.astype(jnp.float32)
    centre = jnp.mean(values, -1, keepdims=True)
    spread = jnp.mean((values - centre) ** 2, -1, keepdims=True)
    return ((values - centre) / jnp.sqrt(spread + 1e-05)).astype(jnp.bfloat16)


def dot(a, b, contract=((1,), (0,))):
    return lax.dot_general(a, b, (contract, ((), ())), preferred_element_type=jnp.float32)


PLACES = 16


def mixing_kernel(tokens, taps, qkv, outer, stream, kept, normed, queries, keys, values, mixed):
    frames, across, channels = tokens.shape
    blocks = across // PLACES
    rows = frames * PLACES
    bf16 = jnp.bfloat16

    def spans(frame):
        for block in range(blocks):
            at = block * rows + frame * PLACES
            yield block * PLACES, at

    for frame in range(frames):
        wide = tokens[frame].astype(jnp.float32)
        summed = taps[1:2, :] * wide
        if frame > 0:
            summed = taps[0:1, :] * tokens[frame - 1].astype(jnp.float32) + summed
        if frame < frames - 1:
            summed = summed + taps[2:3, :] * tokens[frame + 1].astype(jnp.float32)
        stream_one = (wide + summed).astype(bf16)
        unit = layer_normed(stream_one)
        for place, at in spans(frame):
            kept[at : at + PLACES, :] = stream_one[place : place + PLACES, :]
            normed[at : at + PLACES, :] = unit[place : place + PLACES, :]

    width = 256
    head_a = lax.broadcasted_iota(jnp.int32, (width, width), 0) // HD
    head_b = lax.broadcasted_iota(jnp.int32, (width, width), 1) // HD
    same_head = jnp.where(head_a == head_b, 1.0 / HD, 0.0).astype(bf16)

    for target, base in ((queries, 0), (keys, channels)):
        for at in range(0, channels, width):
            part = dot(normed[...], qkv[:, base + at : base + at + width])
            square = part * part
            high = square.astype(bf16)
            low = (square - high.astype(jnp.float32)).astype(bf16)
            mean = dot(high, same_head) + dot(low, same_head)
            target[:, at : at + width] = (part / jnp.sqrt(mean + 1e-06)).astype(bf16)
    for at in range(0, channels, width):
        base = 2 * channels + at
        values[:, at : at + width] = dot(normed[...], qkv[:, base : base + width]).astype(bf16)

    pair = 2 * HD
    first = lax.broadcasted_iota(jnp.int32, (rows, pair), 1) < HD
    place_a = lax.broadcasted_iota(jnp.int32, (rows, 2 * rows), 0) % PLACES
    place_b = lax.broadcasted_iota(jnp.int32, (rows, 2 * rows), 1) % PLACES
    same_place = place_a == place_b
    ones_a = jnp.where(first, 1.0, 0.0).astype(bf16)
    ones_b = jnp.where(first, 0.0, 1.0).astype(bf16)
    ones = jnp.concatenate([ones_a, ones_b], 0)
    for block in range(blocks):
        here = slice(block * rows, (block + 1) * rows)
        for at in range(0, channels, pair):
            query = queries[here, at : at + pair]
            key = keys[here, at : at + pair]
            value = values[here, at : at + pair]
            both = jnp.concatenate([key * ones_a, key * ones_b], 0)
            scores = dot(query, both, ((1,), (1,))) * (1.0 / math.sqrt(HD))
            weights = jnp.where(same_place, jnp.exp(scores), 0.0).astype(bf16)
            both = jnp.concatenate([value * ones_a, value * ones_b], 0)
            summed = dot(weights, jnp.concatenate([both, ones], 1))
            mixed[here, at : at + pair] = (summed[:, :pair] / summed[:, pair:]).astype(bf16)

    attended = dot(mixed[...], outer[...]).astype(bf16).astype(jnp.float32)
    total = (kept[...].astype(jnp.float32) + attended).astype(bf16)
    for frame in range(frames):
        for place, at in spans(frame):
            stream[frame, place : place + PLACES, :] = total[at : at + PLACES, :]


def time_mixing(received, conv_weight, qkv_weight, attn_out_weight):
    frames, across, channels = received.shape
    scratch = pltpu.VMEM((frames * across, channels), jnp.bfloat16)
    return pl.pallas_call(
        mixing_kernel,
        out_shape=jax.ShapeDtypeStruct(received.shape, jnp.bfloat16),
        in_specs=[VMEM] * 4,
        out_specs=VMEM,
        scratch_shapes=[scratch] * 6,
        compiler_params=LIMIT,
        name="mixing",
    )(received, conv_weight, qkv_weight, attn_out_weight)


def dispatch_kernel(
    chips, classes, capacity, place, own, other, own_ids, other_ids, router, *outs
):
    boxes, combs = outs[:chips], outs[chips:]
    tokens = own.shape[0]
    experts = router.shape[0]
    slots = chips * capacity
    chip, core, mine = place[0], place[1], place[2]
    slot = lax.broadcasted_iota(jnp.int32, (slots, tokens), 0)
    target = jnp.bitwise_xor(slot // capacity, chip)
    target = (2 * target + core) * classes + mine
    order = slot % capacity
    before = lax.broadcasted_iota(jnp.int32, (tokens, tokens), 0)
    after = lax.broadcasted_iota(jnp.int32, (tokens, tokens), 1)
    earlier = (before < after).astype(jnp.float32).astype(jnp.bfloat16)
    kinds = lax.broadcasted_iota(jnp.int32, (experts, tokens), 0)
    for side, (rows, ids) in enumerate(((own, own_ids), (other, other_ids))):
        first, second = ids[0:1, :], ids[1:2, :]
        logits = dot(router[...], rows[...], ((1,), (1,)))
        gate_a = jax.nn.sigmoid(
            jnp.sum(jnp.where(kinds == first, logits, 0.0), 0, keepdims=True)
        )
        gate_b = jax.nn.sigmoid(
            jnp.sum(jnp.where(kinds == second, logits, 0.0), 0, keepdims=True)
        )
        whole = gate_a + gate_b
        hit_a, hit_b = target == first, target == second
        member = jnp.where(hit_a | hit_b, 1.0, 0.0)
        rank = dot(member.astype(jnp.bfloat16), earlier)
        taken = jnp.where(rank == order.astype(jnp.float32), member, 0.0)
        share = jnp.where(hit_a, gate_a / whole, gate_b / whole)
        combs[side][...] = (taken * share).astype(jnp.bfloat16)
        moved = dot(taken.astype(jnp.bfloat16), rows[...]).astype(jnp.bfloat16)
        for k in range(chips):
            boxes[k][side * capacity : (side + 1) * capacity, :] = moved[
                k * capacity : (k + 1) * capacity, :
            ]


def dispatched(place, own, other, own_ids, other_ids, router, chips, classes, capacity):
    tokens, channels = own.shape
    bf16 = jnp.bfloat16
    shapes = [jax.ShapeDtypeStruct((2 * capacity, channels), bf16)] * chips
    shapes += [jax.ShapeDtypeStruct((chips * capacity, tokens), bf16)] * 2
    outs = pl.pallas_call(
        functools.partial(dispatch_kernel, chips, classes, capacity),
        out_shape=shapes,
        in_specs=[SMEM] + [VMEM] * 5,
        out_specs=[VMEM] * (chips + 2),
        compiler_params=LIMIT,
        name="dispatch",
    )(place, own, other, own_ids, other_ids, router)
    return outs[:chips], outs[chips:]


def expert_kernel(chips, *refs):
    inputs, (inner, outer) = refs[:chips], refs[chips : chips + 2]
    outputs, (gathered, total) = refs[chips + 2 : 2 * chips + 2], refs[2 * chips + 2 :]
    step, last = pl.program_id(0), pl.num_programs(0) - 1
    size = inputs[0].shape[0]

    @pl.when(step == 0)
    def _():
        for k in range(chips):
            gathered[k * size : (k + 1) * size, :] = inputs[k][...]

    hidden = jax.nn.gelu(dot(gathered[...], inner[0])).astype(jnp.bfloat16)
    part = dot(hidden, outer[0])

    @pl.when(step == 0)
    def _():
        total[...] = part

    @pl.when((step > 0) & (step < last))
    def _():
        total[...] += part

    @pl.when(step == last)
    def _():
        done = (total[...] + part).astype(jnp.bfloat16)
        for k in range(chips):
            outputs[k][...] = done[k * size : (k + 1) * size, :]


def expert_rows(pieces, expert_in, expert_out):
    chips = len(pieces)
    size, channels = pieces[0].shape
    units = expert_in.shape[2]
    tile = units // 4
    whole = pl.BlockSpec((size, channels), lambda i: (0, 0))
    rows = chips * size
    return pl.pallas_call(
        functools.partial(expert_kernel, chips),
        out_shape=[jax.ShapeDtypeStruct((size, channels), jnp.bfloat16)] * chips,
        grid=(units // tile,),
        in_specs=[whole] * chips
        + [
            pl.BlockSpec((1, channels, tile), lambda i: (0, 0, i)),
            pl.BlockSpec((1, tile, channels), lambda i: (0, i, 0)),
        ],
        out_specs=[whole] * chips,
        scratch_shapes=[
            pltpu.VMEM((rows, channels), jnp.bfloat16),
            pltpu.VMEM((rows, channels), jnp.float32),
        ],
        compiler_params=LIMIT,
        cost_estimate=pl.CostEstimate(
            flops=4 * rows * channels * units,
            transcendentals=rows * units,
            bytes_accessed=4 * channels * units,
        ),
        name="experts",
    )(*pieces, *(pltpu.with_memory_space_constraint(w, pltpu.HBM) for w in (expert_in, expert_out)))


def combine_kernel(chips, *refs):
    pieces, combs = refs[:chips], refs[chips : chips + 2]
    own, other = refs[chips + 2 :]
    capacity = pieces[0].shape[0] // 2
    for side, out in enumerate((own, other)):
        rows = jnp.concatenate(
            [pieces[k][side * capacity : (side + 1) * capacity, :] for k in range(chips)], 0
        )
        out[...] = dot(combs[side][...], rows, ((0,), (0,))).astype(out.dtype)


def combined(pieces, combs):
    chips = len(pieces)
    tokens = combs[0].shape[1]
    channels = pieces[0].shape[1]
    return pl.pallas_call(
        functools.partial(combine_kernel, chips),
        out_shape=[
            jax.ShapeDtypeStruct((tokens, channels), jnp.float32),
            jax.ShapeDtypeStruct((tokens, channels), jnp.bfloat16),
        ],
        in_specs=[VMEM] * (chips + 2),
        out_specs=[VMEM] * 2,
        compiler_params=LIMIT,
        name="combine",
    )(*pieces, *combs)


def body(
    tokens,
    conv_weight,
    qkv_weight,
    attn_out_weight,
    router_weight,
    expert_ids,
    expert_in,
    expert_out,
):
    shards = lax.axis_size("tm")
    groups = lax.axis_size("group")
    chips = shards // 2
    classes = groups // 2
    spatial, channels = tokens.shape[1:]
    across = spatial // shards
    experts = router_weight.shape[1]
    capacity = 4 * spatial // experts
    at = lax.axis_index("tm")
    place = jnp.stack([at // 2, at % 2, lax.axis_index("group") // 2]).astype(jnp.int32)

    def swapped(rows, axis, step):
        if step == 0:
            return rows
        size = lax.axis_size(axis)
        return lax.ppermute(rows, axis, [(i, i ^ step) for i in range(size)])

    routed = expert_ids.reshape(spatial, 2).T
    pair = jnp.concatenate([routed, swapped(routed, "tm", 1)], 0)
    ids = [swapped(pair, "group", step) for step in range(groups)]

    received = lax.all_to_all(
        tokens.reshape(1, shards, across, channels),
        "tm",
        split_axis=1,
        concat_axis=0,
        tiled=True,
    ).reshape(shards, across, channels)
    stream_two = time_mixing(received, conv_weight, qkv_weight, attn_out_weight)
    stream = lax.all_to_all(
        stream_two.reshape(shards, 1, across, channels),
        "tm",
        split_axis=0,
        concat_axis=1,
        tiled=True,
    ).reshape(spatial, channels)

    router = router_weight.T
    normed = layer_normed(stream)
    blocks = [normed]
    for step in range(1, groups):
        if step % 2:
            blocks.append(swapped(blocks[step - 1], "group", 1))
        else:
            blocks.append(swapped(normed, "group", step))
    total = stream.astype(jnp.float32)
    for step in range(groups):
        own = blocks[step]
        other = swapped(own, "tm", 1)
        boxes, combs = dispatched(
            place,
            own,
            other,
            ids[step][:2],
            ids[step][2:],
            router,
            chips,
            classes,
            capacity,
        )
        pieces = [swapped(boxes[k], "tm", 2 * k) for k in range(chips)]
        results = expert_rows(pieces, expert_in, expert_out)
        returned = [swapped(results[k], "tm", 2 * k) for k in range(chips)]
        here, there = combined(returned, combs)
        mixed = here + swapped(there, "tm", 1).astype(jnp.float32)
        if step:
            mixed = swapped(mixed.astype(jnp.bfloat16), "group", step)
            mixed = mixed.astype(jnp.float32)
        total = total + mixed
    return total.astype(jnp.bfloat16).reshape(1, spatial, channels)


def solution(mesh):
    placed = (
        P("tm", "group", None),
        P(),
        P(),
        P(),
        P(),
        P("tm", "group", None),
        P(("tm", "group"), None, None),
        P(("tm", "group"), None, None),
    )
    return jax.shard_map(
        body, mesh=mesh, in_specs=placed, out_specs=P("tm", "group", None), check_vma=False
    )
```

```python
import functools
import math

import jax
import jax.numpy as jnp
from jax import lax
from jax.experimental import pallas as pl
from jax.experimental.pallas import tpu as pltpu
from jax.sharding import PartitionSpec as P


HD = 64
VMEM = pl.BlockSpec(memory_space=pltpu.VMEM)
LIMIT = pltpu.CompilerParams(vmem_limit_bytes=12 * 2**20)


def layer_normed(values):
    values = values.astype(jnp.float32)
    centre = jnp.mean(values, -1, keepdims=True)
    spread = jnp.mean((values - centre) ** 2, -1, keepdims=True)
    return ((values - centre) / jnp.sqrt(spread + 1e-05)).astype(jnp.bfloat16)


def dot(a, b, contract=((1,), (0,))):
    return lax.dot_general(a, b, (contract, ((), ())), preferred_element_type=jnp.float32)


PLACES = 16


def mixing_kernel(
    tokens, taps_far, qkv_far, outer_far, inner_far, last_far, stream, inner, last, *scratch
):
    kept, normed, queries, keys, values, mixed, taps, qkv, outer, arrived = scratch
    size = tokens.shape[-1]
    copies = [
        pltpu.make_async_copy(
            qkv_far.at[:, part * size : (part + 1) * size],
            qkv.at[:, part * size : (part + 1) * size],
            arrived.at[part],
        )
        for part in range(3)
    ]
    copies.append(pltpu.make_async_copy(outer_far, outer, arrived.at[3]))
    copies.append(pltpu.make_async_copy(inner_far.at[0], inner, arrived.at[4]))
    copies.append(pltpu.make_async_copy(last_far.at[0], last, arrived.at[5]))
    copies.append(pltpu.make_async_copy(taps_far, taps, arrived.at[6]))
    copies[6].start()
    for copy in copies[:4]:
        copy.start()
    copies[6].wait()
    frames, across, channels = tokens.shape
    blocks = across // PLACES
    rows = frames * PLACES
    bf16 = jnp.bfloat16

    def spans(frame):
        for block in range(blocks):
            at = block * rows + frame * PLACES
            yield block * PLACES, at

    for frame in range(frames):
        wide = tokens[frame].astype(jnp.float32)
        summed = taps[1:2, :] * wide
        if frame > 0:
            summed = taps[0:1, :] * tokens[frame - 1].astype(jnp.float32) + summed
        if frame < frames - 1:
            summed = summed + taps[2:3, :] * tokens[frame + 1].astype(jnp.float32)
        stream_one = (wide + summed).astype(bf16)
        unit = layer_normed(stream_one)
        for place, at in spans(frame):
            kept[at : at + PLACES, :] = stream_one[place : place + PLACES, :]
            normed[at : at + PLACES, :] = unit[place : place + PLACES, :]

    width = 256
    head_a = lax.broadcasted_iota(jnp.int32, (width, width), 0) // HD
    head_b = lax.broadcasted_iota(jnp.int32, (width, width), 1) // HD
    same_head = jnp.where(head_a == head_b, 1.0 / HD, 0.0).astype(bf16)

    for target, base in ((queries, 0), (keys, channels)):
        copies[base // channels].wait()
        for at in range(0, channels, width):
            part = dot(normed[...], qkv[:, base + at : base + at + width])
            square = part * part
            high = square.astype(bf16)
            low = (square - high.astype(jnp.float32)).astype(bf16)
            mean = dot(high, same_head) + dot(low, same_head)
            target[:, at : at + width] = (part / jnp.sqrt(mean + 1e-06)).astype(bf16)
    copies[2].wait()
    copies[4].start()
    copies[5].start()
    for at in range(0, channels, width):
        base = 2 * channels + at
        values[:, at : at + width] = dot(normed[...], qkv[:, base : base + width]).astype(bf16)

    pair = 2 * HD
    first = lax.broadcasted_iota(jnp.int32, (rows, pair), 1) < HD
    place_a = lax.broadcasted_iota(jnp.int32, (rows, 2 * rows), 0) % PLACES
    place_b = lax.broadcasted_iota(jnp.int32, (rows, 2 * rows), 1) % PLACES
    same_place = place_a == place_b
    ones_a = jnp.where(first, 1.0, 0.0).astype(bf16)
    ones_b = jnp.where(first, 0.0, 1.0).astype(bf16)
    ones = jnp.concatenate([ones_a, ones_b], 0)
    for block in range(blocks):
        here = slice(block * rows, (block + 1) * rows)
        for at in range(0, channels, pair):
            query = queries[here, at : at + pair]
            key = keys[here, at : at + pair]
            value = values[here, at : at + pair]
            both = jnp.concatenate([key * ones_a, key * ones_b], 0)
            scores = dot(query, both, ((1,), (1,))) * (1.0 / math.sqrt(HD))
            weights = jnp.where(same_place, jnp.exp(scores), 0.0).astype(bf16)
            both = jnp.concatenate([value * ones_a, value * ones_b], 0)
            summed = dot(weights, jnp.concatenate([both, ones], 1))
            mixed[here, at : at + pair] = (summed[:, :pair] / summed[:, pair:]).astype(bf16)

    copies[3].wait()
    attended = dot(mixed[...], outer[...]).astype(bf16).astype(jnp.float32)
    total = (kept[...].astype(jnp.float32) + attended).astype(bf16)
    for frame in range(frames):
        for place, at in spans(frame):
            stream[frame, place : place + PLACES, :] = total[at : at + PLACES, :]
    copies[4].wait()
    copies[5].wait()


def time_mixing(received, conv_weight, qkv_weight, attn_out_weight, expert_in, expert_out):
    frames, across, channels = received.shape
    bf16 = jnp.bfloat16
    rows = pltpu.VMEM((frames * across, channels), bf16)
    far = pl.BlockSpec(memory_space=pltpu.HBM)
    return pl.pallas_call(
        mixing_kernel,
        out_shape=[
            jax.ShapeDtypeStruct(received.shape, bf16),
            jax.ShapeDtypeStruct(expert_in.shape[1:], bf16),
            jax.ShapeDtypeStruct(expert_out.shape[1:], bf16),
        ],
        in_specs=[VMEM] + [far] * 5,
        out_specs=[VMEM] * 3,
        scratch_shapes=[rows] * 6
        + [
            pltpu.VMEM(conv_weight.shape, jnp.float32),
            pltpu.VMEM(qkv_weight.shape, bf16),
            pltpu.VMEM(attn_out_weight.shape, bf16),
            pltpu.SemaphoreType.DMA((7,)),
        ],
        compiler_params=pltpu.CompilerParams(vmem_limit_bytes=40 * 2**20),
        name="mixing",
    )(
        received,
        *(
            pltpu.with_memory_space_constraint(part, pltpu.HBM)
            for part in (conv_weight, qkv_weight, attn_out_weight, expert_in, expert_out)
        ),
    )


def dispatch_kernel(
    chips, classes, capacity, own, other, own_ids, other_ids, router, *outs
):
    boxes, combs = outs[:chips], outs[chips:]
    tokens = own.shape[0]
    experts = router.shape[0]
    slots = chips * capacity
    at = lax.axis_index("tm")
    chip, core, mine = at // 2, at % 2, lax.axis_index("group") // 2
    slot = lax.broadcasted_iota(jnp.int32, (slots, tokens), 0)
    target = jnp.bitwise_xor(slot // capacity, chip)
    target = (2 * target + core) * classes + mine
    order = slot % capacity
    before = lax.broadcasted_iota(jnp.int32, (tokens, tokens), 0)
    after = lax.broadcasted_iota(jnp.int32, (tokens, tokens), 1)
    earlier = (before < after).astype(jnp.float32).astype(jnp.bfloat16)
    kinds = lax.broadcasted_iota(jnp.int32, (experts, tokens), 0)
    for side, (rows, ids) in enumerate(((own, own_ids), (other, other_ids))):
        first, second = ids[0:1, :], ids[1:2, :]
        logits = dot(router[...], rows[...], ((1,), (1,)))
        gate_a = jax.nn.sigmoid(
            jnp.sum(jnp.where(kinds == first, logits, 0.0), 0, keepdims=True)
        )
        gate_b = jax.nn.sigmoid(
            jnp.sum(jnp.where(kinds == second, logits, 0.0), 0, keepdims=True)
        )
        whole = gate_a + gate_b
        hit_a, hit_b = target == first, target == second
        member = jnp.where(hit_a | hit_b, 1.0, 0.0)
        rank = dot(member.astype(jnp.bfloat16), earlier)
        taken = jnp.where(rank == order.astype(jnp.float32), member, 0.0)
        share = jnp.where(hit_a, gate_a / whole, gate_b / whole)
        combs[side][...] = (taken * share).astype(jnp.bfloat16)
        moved = dot(taken.astype(jnp.bfloat16), rows[...]).astype(jnp.bfloat16)
        for k in range(chips):
            boxes[k][side * capacity : (side + 1) * capacity, :] = moved[
                k * capacity : (k + 1) * capacity, :
            ]


def dispatched(own, other, own_ids, other_ids, router, chips, classes, capacity):
    tokens, channels = own.shape
    bf16 = jnp.bfloat16
    shapes = [jax.ShapeDtypeStruct((2 * capacity, channels), bf16)] * chips
    shapes += [jax.ShapeDtypeStruct((chips * capacity, tokens), bf16)] * 2
    outs = pl.pallas_call(
        functools.partial(dispatch_kernel, chips, classes, capacity),
        out_shape=shapes,
        in_specs=[VMEM] * 5,
        out_specs=[VMEM] * (chips + 2),
        compiler_params=LIMIT,
        name="dispatch",
    )(own, other, own_ids, other_ids, router)
    return outs[:chips], outs[chips:]


def expert_kernel(chips, *refs):
    inputs, (inner, outer) = refs[:chips], refs[chips : chips + 2]
    outputs, (gathered, total) = refs[chips + 2 : -2], refs[-2:]
    size = inputs[0].shape[0]
    units = inner.shape[1]
    tile = units // 4
    for k in range(chips):
        gathered[k * size : (k + 1) * size, :] = inputs[k][...]
    for at in range(0, units, tile):
        hidden = jax.nn.gelu(dot(gathered[...], inner[:, at : at + tile])).astype(jnp.bfloat16)
        part = dot(hidden, outer[at : at + tile, :])
        if at == 0:
            total[...] = part
        elif at + tile < units:
            total[...] += part
        else:
            done = (total[...] + part).astype(jnp.bfloat16)
            step = outputs[0].shape[0]
            for k, out in enumerate(outputs):
                out[...] = done[k * step : (k + 1) * step, :]


def expert_rows(pieces, inner, outer, joined):
    chips = len(pieces)
    size, channels = pieces[0].shape
    units = inner.shape[1]
    rows = chips * size
    count = 1 if joined else chips
    return pl.pallas_call(
        functools.partial(expert_kernel, chips),
        out_shape=[jax.ShapeDtypeStruct((rows // count, channels), jnp.bfloat16)] * count,
        in_specs=[VMEM] * (chips + 2),
        out_specs=[VMEM] * count,
        scratch_shapes=[
            pltpu.VMEM((rows, channels), jnp.bfloat16),
            pltpu.VMEM((rows, channels), jnp.float32),
        ],
        compiler_params=pltpu.CompilerParams(vmem_limit_bytes=20 * 2**20),
        cost_estimate=pl.CostEstimate(
            flops=4 * rows * channels * units,
            transcendentals=rows * units,
            bytes_accessed=4 * channels * units,
        ),
        name="experts",
    )(*pieces, inner, outer)


def pair_kernel(one, two, *outs):
    size = outs[0].shape[0]
    for k, out in enumerate(outs):
        at = slice(k * size, (k + 1) * size)
        out[...] = (one[at, :].astype(jnp.float32) + two[at, :].astype(jnp.float32)).astype(
            out.dtype
        )


def pair_summed(one, two, chips):
    rows, channels = one.shape
    return pl.pallas_call(
        pair_kernel,
        out_shape=[jax.ShapeDtypeStruct((rows // chips, channels), one.dtype)] * chips,
        in_specs=[VMEM] * 2,
        out_specs=[VMEM] * chips,
        compiler_params=LIMIT,
        name="pair",
    )(one, two)


def combine_kernel(chips, *refs):
    pieces, combs = refs[:chips], refs[chips : chips + 2]
    own, other = refs[chips + 2 :]
    capacity = pieces[0].shape[0] // 2
    for side, out in enumerate((own, other)):
        rows = jnp.concatenate(
            [pieces[k][side * capacity : (side + 1) * capacity, :] for k in range(chips)], 0
        )
        out[...] = dot(combs[side][...], rows, ((0,), (0,))).astype(out.dtype)


def combined(pieces, combs):
    chips = len(pieces)
    tokens = combs[0].shape[1]
    channels = pieces[0].shape[1]
    return pl.pallas_call(
        functools.partial(combine_kernel, chips),
        out_shape=[
            jax.ShapeDtypeStruct((tokens, channels), jnp.float32),
            jax.ShapeDtypeStruct((tokens, channels), jnp.bfloat16),
        ],
        in_specs=[VMEM] * (chips + 2),
        out_specs=[VMEM] * 2,
        compiler_params=LIMIT,
        name="combine",
    )(*pieces, *combs)


def norm_kernel(rows, out):
    out[...] = layer_normed(rows[...])


def row_normed(rows):
    return pl.pallas_call(
        norm_kernel,
        out_shape=jax.ShapeDtypeStruct(rows.shape, rows.dtype),
        in_specs=[VMEM],
        out_specs=VMEM,
        compiler_params=LIMIT,
        name="norm",
    )(rows)


def sum_kernel(halves, *refs):
    whole, (first, second), out = refs[:-1], halves, refs[-1]
    half = out.shape[0] // 2
    parts, whole = whole[-(first + second) :], whole[: -(first + second)]
    for at, group in ((0, parts[:first]), (half, parts[first:])):
        total = whole[0][at : at + half, :].astype(jnp.float32)
        for part in whole[1:]:
            total = total + part[at : at + half, :].astype(jnp.float32)
        for part in group:
            total = total + part[...].astype(jnp.float32)
        out[at : at + half, :] = total.astype(out.dtype)


def summed(whole, first, second):
    rows = [*whole, *first, *second]
    return pl.pallas_call(
        functools.partial(sum_kernel, (len(first), len(second))),
        out_shape=jax.ShapeDtypeStruct(whole[0].shape, whole[0].dtype),
        in_specs=[VMEM] * len(rows),
        out_specs=VMEM,
        compiler_params=LIMIT,
        name="total",
    )(*rows)


def body(
    tokens,
    conv_weight,
    qkv_weight,
    attn_out_weight,
    router_weight,
    expert_ids,
    expert_in,
    expert_out,
):
    shards = lax.axis_size("tm")
    groups = lax.axis_size("group")
    chips = shards // 2
    classes = groups // 2
    spatial, channels = tokens.shape[1:]
    across = spatial // shards
    experts = router_weight.shape[1]
    capacity = 4 * spatial // experts

    def swapped(rows, axis, step):
        if step == 0:
            return rows
        size = lax.axis_size(axis)
        return lax.ppermute(rows, axis, [(i, i ^ step) for i in range(size)])

    routed = expert_ids.reshape(spatial, 2).T
    pair = jnp.concatenate([routed, swapped(routed, "tm", 1)], 0)
    blocked = [step for step in range(groups) if step != 1]
    ids = {step: swapped(pair, "group", step) for step in blocked}

    received = lax.all_to_all(
        tokens.reshape(1, shards, across, channels),
        "tm",
        split_axis=1,
        concat_axis=0,
        tiled=True,
    ).reshape(shards, across, channels)
    stream_two, inner, outer = time_mixing(
        received, conv_weight, qkv_weight, attn_out_weight, expert_in, expert_out
    )
    stream = lax.all_to_all(
        stream_two.reshape(shards, 1, across, channels),
        "tm",
        split_axis=0,
        concat_axis=1,
        tiled=True,
    ).reshape(spatial, channels)

    router = router_weight.T
    normed = row_normed(stream)
    blocks = {0: normed}
    for step in blocked[1:]:
        if step % 2:
            blocks[step] = swapped(blocks[step - 1], "group", 1)
        else:
            blocks[step] = swapped(normed, "group", step)
    whole, first, second, waiting = [stream], [], [], None
    half = spatial // 2
    bf16 = jnp.bfloat16
    for step in blocked:
        own = blocks[step]
        other = swapped(own, "tm", 1)
        boxes, combs = dispatched(
            own,
            other,
            ids[step][:2],
            ids[step][2:],
            router,
            chips,
            classes,
            capacity,
        )
        pieces = [swapped(boxes[k], "tm", 2 * k) for k in range(chips)]
        results = expert_rows(pieces, inner, outer, step == 0)
        if step == 0:
            near = [swapped(pieces[k], "group", 1) for k in range(chips)]
            others = expert_rows(near, inner, outer, True)
            others = swapped(others[0], "group", 1)
            results = pair_summed(results[0], others, chips)
        returned = [swapped(results[k], "tm", 2 * k) for k in range(chips)]
        here, there = combined(returned, combs)
        across_core = swapped(there, "tm", 1)
        if step == 0:
            whole += [here, across_core]
            continue
        mixed = here + across_core.astype(jnp.float32)
        first.append(swapped(mixed[:half].astype(bf16), "group", step))
        if step % 2 == 0:
            waiting = mixed[half:]
        else:
            near = swapped(mixed[half:].astype(bf16), "group", 1)
            joint = (waiting + near.astype(jnp.float32)).astype(bf16)
            second.append(swapped(joint, "group", step - 1))
    return summed(whole, first, second).reshape(1, spatial, channels)


def solution(mesh):
    placed = (
        P("tm", "group", None),
        P(),
        P(),
        P(),
        P(),
        P("tm", "group", None),
        P(("tm", "group"), None, None),
        P(("tm", "group"), None, None),
    )
    return jax.shard_map(
        body, mesh=mesh, in_specs=placed, out_specs=P("tm", "group", None), check_vma=False
    )
```

```python
import functools
import math

import jax
import jax.numpy as jnp
from jax import lax
from jax.experimental import pallas as pl
from jax.experimental.pallas import tpu as pltpu
from jax.sharding import PartitionSpec as P


HD = 64
VMEM = pl.BlockSpec(memory_space=pltpu.VMEM)
LIMIT = pltpu.CompilerParams(vmem_limit_bytes=12 * 2**20)


def layer_normed(values):
    values = values.astype(jnp.float32)
    centre = jnp.mean(values, -1, keepdims=True)
    spread = jnp.mean((values - centre) ** 2, -1, keepdims=True)
    return ((values - centre) / jnp.sqrt(spread + 1e-05)).astype(jnp.bfloat16)


def dot(a, b, contract=((1,), (0,))):
    return lax.dot_general(a, b, (contract, ((), ())), preferred_element_type=jnp.float32)


PLACES = 16


def mixing_kernel(
    tokens, taps, outer, qkv_far, *refs
):
    pieces = refs[:-8]
    kept, normed, queries, keys, values, mixed, qkv, arrived = refs[-8:]
    size = tokens.shape[-1]
    copies = [
        pltpu.make_async_copy(
            qkv_far.at[:, part * size : (part + 1) * size],
            qkv.at[:, part * size : (part + 1) * size],
            arrived.at[part],
        )
        for part in range(3)
    ]
    copies[0].start()
    frames, across, channels = tokens.shape
    blocks = across // PLACES
    rows = frames * PLACES
    bf16 = jnp.bfloat16

    def spans(frame):
        for block in range(blocks):
            at = block * rows + frame * PLACES
            yield block * PLACES, at

    for frame in range(frames):
        wide = tokens[frame].astype(jnp.float32)
        summed = taps[1:2, :] * wide
        if frame > 0:
            summed = taps[0:1, :] * tokens[frame - 1].astype(jnp.float32) + summed
        if frame < frames - 1:
            summed = summed + taps[2:3, :] * tokens[frame + 1].astype(jnp.float32)
        stream_one = (wide + summed).astype(bf16)
        unit = layer_normed(stream_one)
        for place, at in spans(frame):
            kept[at : at + PLACES, :] = stream_one[place : place + PLACES, :]
            normed[at : at + PLACES, :] = unit[place : place + PLACES, :]

    copies[1].start()
    copies[2].start()
    width = 256
    head_a = lax.broadcasted_iota(jnp.int32, (width, width), 0) // HD
    head_b = lax.broadcasted_iota(jnp.int32, (width, width), 1) // HD
    same_head = jnp.where(head_a == head_b, 1.0 / HD, 0.0).astype(bf16)

    for target, base in ((queries, 0), (keys, channels)):
        copies[base // channels].wait()
        for at in range(0, channels, width):
            part = dot(normed[...], qkv[:, base + at : base + at + width])
            square = part * part
            high = square.astype(bf16)
            low = (square - high.astype(jnp.float32)).astype(bf16)
            mean = dot(high, same_head) + dot(low, same_head)
            target[:, at : at + width] = (part / jnp.sqrt(mean + 1e-06)).astype(bf16)
    copies[2].wait()
    for at in range(0, channels, width):
        base = 2 * channels + at
        values[:, at : at + width] = dot(normed[...], qkv[:, base : base + width]).astype(bf16)

    pair = 2 * HD
    first = lax.broadcasted_iota(jnp.int32, (rows, pair), 1) < HD
    place_a = lax.broadcasted_iota(jnp.int32, (rows, 2 * rows), 0) % PLACES
    place_b = lax.broadcasted_iota(jnp.int32, (rows, 2 * rows), 1) % PLACES
    same_place = place_a == place_b
    ones_a = jnp.where(first, 1.0, 0.0).astype(bf16)
    ones_b = jnp.where(first, 0.0, 1.0).astype(bf16)
    ones = jnp.concatenate([ones_a, ones_b], 0)
    for block in range(blocks):
        here = slice(block * rows, (block + 1) * rows)
        for at in range(0, channels, pair):
            query = queries[here, at : at + pair]
            key = keys[here, at : at + pair]
            value = values[here, at : at + pair]
            both = jnp.concatenate([key * ones_a, key * ones_b], 0)
            scores = dot(query, both, ((1,), (1,))) * (1.0 / math.sqrt(HD))
            weights = jnp.where(same_place, jnp.exp(scores), 0.0).astype(bf16)
            both = jnp.concatenate([value * ones_a, value * ones_b], 0)
            summed = dot(weights, jnp.concatenate([both, ones], 1))
            mixed[here, at : at + pair] = (summed[:, :pair] / summed[:, pair:]).astype(bf16)

    attended = dot(mixed[...], outer[...]).astype(bf16).astype(jnp.float32)
    kept[...] = (kept[...].astype(jnp.float32) + attended).astype(bf16)
    chip = lax.axis_index("tm") // 2
    for k, piece in enumerate(pieces):
        for side in range(2):
            frame = 2 * jnp.bitwise_xor(chip, k) + side
            for block in range(blocks):
                at = pl.multiple_of(block * rows + frame * PLACES, PLACES)
                to = side * across + block * PLACES
                piece[to : to + PLACES, :] = kept[pl.ds(at, PLACES), :]


def fetch_kernel(count, *refs):
    arrived = refs[-1]
    copies = [
        pltpu.make_async_copy(refs[at], refs[count + at], arrived.at[at]) for at in range(count)
    ]
    for copy in copies:
        copy.start()
    for copy in copies:
        copy.wait()


def fetched(*parts):
    return pl.pallas_call(
        functools.partial(fetch_kernel, len(parts)),
        out_shape=[jax.ShapeDtypeStruct(part.shape, part.dtype) for part in parts],
        in_specs=[pl.BlockSpec(memory_space=pltpu.HBM)] * len(parts),
        out_specs=[VMEM] * len(parts),
        scratch_shapes=[pltpu.SemaphoreType.DMA((len(parts),))],
        compiler_params=pltpu.CompilerParams(vmem_limit_bytes=2**20),
        name="fetch",
    )(*(pltpu.with_memory_space_constraint(part, pltpu.HBM) for part in parts))


def time_mixing(received, conv_weight, qkv_weight, attn_out_weight):
    frames, across, channels = received.shape
    bf16 = jnp.bfloat16
    rows = pltpu.VMEM((frames * across, channels), bf16)
    far = pl.BlockSpec(memory_space=pltpu.HBM)
    return pl.pallas_call(
        mixing_kernel,
        out_shape=[jax.ShapeDtypeStruct((2 * across, channels), bf16)] * (frames // 2),
        in_specs=[VMEM] * 3 + [far],
        out_specs=[VMEM] * (frames // 2),
        scratch_shapes=[rows] * 6
        + [pltpu.VMEM(qkv_weight.shape, bf16), pltpu.SemaphoreType.DMA((3,))],
        compiler_params=pltpu.CompilerParams(vmem_limit_bytes=28 * 2**20),
        name="mixing",
    )(
        received,
        conv_weight,
        attn_out_weight,
        pltpu.with_memory_space_constraint(qkv_weight, pltpu.HBM),
    )


def dispatch_kernel(
    chips, classes, capacity, parts, own_ids, other_ids, router, *refs
):
    own, other, outs = refs[:parts], refs[parts : 2 * parts], refs[2 * parts :]
    boxes, combs = outs[:chips], outs[chips:]
    tokens = own_ids.shape[1]
    experts = router.shape[0]
    slots = chips * capacity
    at = lax.axis_index("tm")
    chip, core, mine = at // 2, at % 2, lax.axis_index("group") // 2
    slot = lax.broadcasted_iota(jnp.int32, (slots, tokens), 0)
    target = jnp.bitwise_xor(slot // capacity, chip)
    target = (2 * target + core) * classes + mine
    order = slot % capacity
    before = lax.broadcasted_iota(jnp.int32, (tokens, tokens), 0)
    after = lax.broadcasted_iota(jnp.int32, (tokens, tokens), 1)
    earlier = (before < after).astype(jnp.float32).astype(jnp.bfloat16)
    kinds = lax.broadcasted_iota(jnp.int32, (experts, tokens), 0)
    for side, (pieces, ids) in enumerate(((own, own_ids), (other, other_ids))):
        rows = jnp.concatenate([piece[...] for piece in pieces], 0)
        first, second = ids[0:1, :], ids[1:2, :]
        logits = dot(router[...], rows, ((1,), (1,)))
        gate_a = jax.nn.sigmoid(
            jnp.sum(jnp.where(kinds == first, logits, 0.0), 0, keepdims=True)
        )
        gate_b = jax.nn.sigmoid(
            jnp.sum(jnp.where(kinds == second, logits, 0.0), 0, keepdims=True)
        )
        whole = gate_a + gate_b
        hit_a, hit_b = target == first, target == second
        member = jnp.where(hit_a | hit_b, 1.0, 0.0)
        rank = dot(member.astype(jnp.bfloat16), earlier)
        taken = jnp.where(rank == order.astype(jnp.float32), member, 0.0)
        share = jnp.where(hit_a, gate_a / whole, gate_b / whole)
        combs[side][...] = (taken * share).astype(jnp.bfloat16)
        moved = dot(taken.astype(jnp.bfloat16), rows).astype(jnp.bfloat16)
        for k in range(chips):
            boxes[k][side * capacity : (side + 1) * capacity, :] = moved[
                k * capacity : (k + 1) * capacity, :
            ]


def dispatched(own, other, own_ids, other_ids, router, chips, classes, capacity):
    tokens, channels = own_ids.shape[1], own[0].shape[1]
    bf16 = jnp.bfloat16
    shapes = [jax.ShapeDtypeStruct((2 * capacity, channels), bf16)] * chips
    shapes += [jax.ShapeDtypeStruct((chips * capacity, tokens), bf16)] * 2
    outs = pl.pallas_call(
        functools.partial(dispatch_kernel, chips, classes, capacity, len(own)),
        out_shape=shapes,
        in_specs=[VMEM] * (3 + 2 * len(own)),
        out_specs=[VMEM] * (chips + 2),
        compiler_params=LIMIT,
        name="dispatch",
    )(own_ids, other_ids, router, *own, *other)
    return outs[:chips], outs[chips:]


def expert_kernel(chips, *refs):
    inputs, (inner, outer) = refs[:chips], refs[chips : chips + 2]
    outputs, (gathered, total) = refs[chips + 2 : -2], refs[-2:]
    size = inputs[0].shape[0]
    units = inner.shape[1]
    tile = units // 4
    for k in range(chips):
        gathered[k * size : (k + 1) * size, :] = inputs[k][...]
    for at in range(0, units, tile):
        hidden = jax.nn.gelu(dot(gathered[...], inner[:, at : at + tile])).astype(jnp.bfloat16)
        part = dot(hidden, outer[at : at + tile, :])
        if at == 0:
            total[...] = part
        elif at + tile < units:
            total[...] += part
        else:
            done = (total[...] + part).astype(jnp.bfloat16)
            step = outputs[0].shape[0]
            for k, out in enumerate(outputs):
                out[...] = done[k * step : (k + 1) * step, :]


def expert_rows(pieces, inner, outer, joined):
    chips = len(pieces)
    size, channels = pieces[0].shape
    units = inner.shape[1]
    rows = chips * size
    count = 1 if joined else chips
    return pl.pallas_call(
        functools.partial(expert_kernel, chips),
        out_shape=[jax.ShapeDtypeStruct((rows // count, channels), jnp.bfloat16)] * count,
        in_specs=[VMEM] * (chips + 2),
        out_specs=[VMEM] * count,
        scratch_shapes=[
            pltpu.VMEM((rows, channels), jnp.bfloat16),
            pltpu.VMEM((rows, channels), jnp.float32),
        ],
        compiler_params=pltpu.CompilerParams(vmem_limit_bytes=20 * 2**20),
        cost_estimate=pl.CostEstimate(
            flops=4 * rows * channels * units,
            transcendentals=rows * units,
            bytes_accessed=4 * channels * units,
        ),
        name="experts",
    )(*pieces, inner, outer)


def pair_kernel(first, one, two, *outs):
    size = outs[0].shape[0]
    for k, out in enumerate(outs):
        both = one[(first + k) * size : (first + k + 1) * size, :].astype(jnp.float32)
        both = both + two[k * size : (k + 1) * size, :].astype(jnp.float32)
        out[...] = both.astype(out.dtype)


def pair_summed(one, two, first, count):
    rows, channels = two.shape
    return pl.pallas_call(
        functools.partial(pair_kernel, first),
        out_shape=[jax.ShapeDtypeStruct((rows // count, channels), one.dtype)] * count,
        in_specs=[VMEM] * 2,
        out_specs=[VMEM] * count,
        compiler_params=LIMIT,
        name="pair",
    )(one, two)


def combine_kernel(chips, *refs):
    pieces, combs = refs[:chips], refs[chips : chips + 2]
    own, other = refs[chips + 2 :]
    capacity = pieces[0].shape[0] // 2
    for side, out in enumerate((own, other)):
        rows = jnp.concatenate(
            [pieces[k][side * capacity : (side + 1) * capacity, :] for k in range(chips)], 0
        )
        out[...] = dot(combs[side][...], rows, ((0,), (0,))).astype(out.dtype)


def combined(pieces, combs):
    chips = len(pieces)
    tokens = combs[0].shape[1]
    channels = pieces[0].shape[1]
    return pl.pallas_call(
        functools.partial(combine_kernel, chips),
        out_shape=[
            jax.ShapeDtypeStruct((tokens, channels), jnp.float32),
            jax.ShapeDtypeStruct((tokens, channels), jnp.bfloat16),
        ],
        in_specs=[VMEM] * (chips + 2),
        out_specs=[VMEM] * 2,
        compiler_params=LIMIT,
        name="combine",
    )(*pieces, *combs)


def norm_kernel(chips, *refs):
    sides, (stream, own, other) = (refs[:chips], refs[chips : 2 * chips]), refs[2 * chips :]
    at = lax.axis_index("tm")
    chip, core = at // 2, at % 2
    across = refs[0].shape[0] // 2
    for k in range(chips):
        for far, pieces in enumerate(sides):
            block = 2 * jnp.bitwise_xor(chip, k) + (1 - core if far else core)
            to = pl.ds(pl.multiple_of(block * across, across), across)
            rows = pieces[k][pl.ds(pl.multiple_of(core * across, across), across), :]
            stream[to, :] = rows
            own[to, :] = layer_normed(rows)
            rows = pieces[k][pl.ds(pl.multiple_of((1 - core) * across, across), across), :]
            other[to, :] = layer_normed(rows)


def rows_normed(mine, theirs):
    chips = len(mine)
    size, channels = mine[0].shape
    return pl.pallas_call(
        functools.partial(norm_kernel, chips),
        out_shape=[jax.ShapeDtypeStruct((chips * size, channels), mine[0].dtype)] * 3,
        in_specs=[VMEM] * (2 * chips),
        out_specs=[VMEM] * 3,
        compiler_params=LIMIT,
        name="norm",
    )(*mine, *theirs)


def sum_kernel(halves, *refs):
    whole, (first, second), out = refs[:-1], halves, refs[-1]
    half = out.shape[0] // 2
    parts, whole = whole[-(first + second) :], whole[: -(first + second)]
    for at, group in ((0, parts[:first]), (half, parts[first:])):
        total = whole[0][at : at + half, :].astype(jnp.float32)
        for part in whole[1:]:
            total = total + part[at : at + half, :].astype(jnp.float32)
        for part in group:
            total = total + part[...].astype(jnp.float32)
        out[at : at + half, :] = total.astype(out.dtype)


def summed(whole, first, second):
    rows = [*whole, *first, *second]
    return pl.pallas_call(
        functools.partial(sum_kernel, (len(first), len(second))),
        out_shape=jax.ShapeDtypeStruct(whole[0].shape, whole[0].dtype),
        in_specs=[VMEM] * len(rows),
        out_specs=VMEM,
        compiler_params=LIMIT,
        name="total",
    )(*rows)


def body(
    tokens,
    conv_weight,
    qkv_weight,
    attn_out_weight,
    router_weight,
    expert_ids,
    expert_in,
    expert_out,
):
    shards = lax.axis_size("tm")
    groups = lax.axis_size("group")
    chips = shards // 2
    classes = groups // 2
    spatial, channels = tokens.shape[1:]
    across = spatial // shards
    experts = router_weight.shape[1]
    capacity = 4 * spatial // experts

    def swapped(rows, axis, step):
        if step == 0:
            return rows
        size = lax.axis_size(axis)
        return lax.ppermute(rows, axis, [(i, i ^ step) for i in range(size)])

    routed = expert_ids.reshape(spatial, 2).T
    pair = jnp.concatenate([routed, swapped(routed, "tm", 1)], 0)
    blocked = [step for step in range(groups) if step != 1]
    ids = {step: swapped(pair, "group", step) for step in blocked}

    received = lax.all_to_all(
        tokens.reshape(1, shards, across, channels),
        "tm",
        split_axis=1,
        concat_axis=0,
        tiled=True,
    ).reshape(shards, across, channels)
    conv_weight, attn_out_weight = fetched(conv_weight, attn_out_weight)
    pieces = time_mixing(received, conv_weight, qkv_weight, attn_out_weight)
    inner, outer = fetched(expert_in[0], expert_out[0])
    mine = [swapped(pieces[k], "tm", 2 * k) for k in range(chips)]
    theirs = [swapped(mine[k], "tm", 1) for k in range(chips)]
    stream, normed, beside = rows_normed(mine, theirs)

    router = router_weight.T
    blocks = {0: (normed,)}
    for step in blocked[1:]:
        sources = blocks[step - 1] if step % 2 else blocks[0]
        blocks[step] = tuple(swapped(rows, "group", 1 if step % 2 else step) for rows in sources)
    whole, first, second, waiting = [stream], [], [], None
    half = spatial // 2
    bf16 = jnp.bfloat16
    for step in blocked:
        own = blocks[step]
        other = tuple(swapped(rows, "tm", 1) for rows in own)
        other = other if step else (beside,)
        boxes, combs = dispatched(
            own,
            other,
            ids[step][:2],
            ids[step][2:],
            router,
            chips,
            classes,
            capacity,
        )
        pieces = [swapped(boxes[k], "tm", 2 * k) for k in range(chips)]
        results = expert_rows(pieces, inner, outer, step == 0)
        if step == 0:
            near = [swapped(pieces[k], "group", 1) for k in range(chips)]
            joined, results = results[0], []
            for at in (0, chips // 2):
                others = expert_rows(near[at : at + chips // 2], inner, outer, True)
                others = swapped(others[0], "group", 1)
                results += pair_summed(joined, others, at, chips // 2)
        returned = [swapped(results[k], "tm", 2 * k) for k in range(chips)]
        here, there = combined(returned, combs)
        across_core = swapped(there, "tm", 1)
        if step == 0:
            whole += [here, across_core]
            continue
        mixed = here + across_core.astype(jnp.float32)
        first.append(swapped(mixed[:half].astype(bf16), "group", step))
        if step % 2 == 0:
            waiting = mixed[half:]
        else:
            near = swapped(mixed[half:].astype(bf16), "group", 1)
            joint = (waiting + near.astype(jnp.float32)).astype(bf16)
            second.append(swapped(joint, "group", step - 1))
    return summed(whole, first, second).reshape(1, spatial, channels)


def solution(mesh):
    placed = (
        P("tm", "group", None),
        P(),
        P(),
        P(),
        P(),
        P("tm", "group", None),
        P(("tm", "group"), None, None),
        P(("tm", "group"), None, None),
    )
    return jax.shard_map(
        body, mesh=mesh, in_specs=placed, out_specs=P("tm", "group", None), check_vma=False
    )
```

```python
import functools
import math

import jax
import jax.numpy as jnp
from jax import lax
from jax.experimental import pallas as pl
from jax.experimental.pallas import tpu as pltpu
from jax.sharding import PartitionSpec as P


HD = 64
VMEM = pl.BlockSpec(memory_space=pltpu.VMEM)
LIMIT = pltpu.CompilerParams(vmem_limit_bytes=12 * 2**20)


def layer_normed(values):
    values = values.astype(jnp.float32)
    centre = jnp.mean(values, -1, keepdims=True)
    spread = jnp.mean((values - centre) ** 2, -1, keepdims=True)
    return ((values - centre) / jnp.sqrt(spread + 1e-05)).astype(jnp.bfloat16)


def dot(a, b, contract=((1,), (0,))):
    return lax.dot_general(a, b, (contract, ((), ())), preferred_element_type=jnp.float32)


PLACES = 16


def mixing_kernel(
    tokens, taps, outer, qkv_far, *refs
):
    pieces = refs[:-8]
    kept, normed, queries, keys, values, mixed, qkv, arrived = refs[-8:]
    size = tokens.shape[-1]
    copies = [
        pltpu.make_async_copy(
            qkv_far.at[:, part * size : (part + 1) * size],
            qkv.at[:, part * size : (part + 1) * size],
            arrived.at[part],
        )
        for part in range(3)
    ]
    copies[0].start()
    frames, across, channels = tokens.shape
    blocks = across // PLACES
    rows = frames * PLACES
    bf16 = jnp.bfloat16

    def spans(frame):
        for block in range(blocks):
            at = block * rows + frame * PLACES
            yield block * PLACES, at

    for frame in range(frames):
        wide = tokens[frame].astype(jnp.float32)
        summed = taps[1:2, :] * wide
        if frame > 0:
            summed = taps[0:1, :] * tokens[frame - 1].astype(jnp.float32) + summed
        if frame < frames - 1:
            summed = summed + taps[2:3, :] * tokens[frame + 1].astype(jnp.float32)
        stream_one = (wide + summed).astype(bf16)
        unit = layer_normed(stream_one)
        for place, at in spans(frame):
            kept[at : at + PLACES, :] = stream_one[place : place + PLACES, :]
            normed[at : at + PLACES, :] = unit[place : place + PLACES, :]

    copies[1].start()
    copies[2].start()
    width = 256
    head_a = lax.broadcasted_iota(jnp.int32, (width, width), 0) // HD
    head_b = lax.broadcasted_iota(jnp.int32, (width, width), 1) // HD
    same_head = jnp.where(head_a == head_b, 1.0 / HD, 0.0).astype(bf16)

    for target, base in ((queries, 0), (keys, channels)):
        copies[base // channels].wait()
        for at in range(0, channels, width):
            part = dot(normed[...], qkv[:, base + at : base + at + width])
            square = part * part
            high = square.astype(bf16)
            low = (square - high.astype(jnp.float32)).astype(bf16)
            mean = dot(high, same_head) + dot(low, same_head)
            target[:, at : at + width] = (part / jnp.sqrt(mean + 1e-06)).astype(bf16)
    copies[2].wait()
    for at in range(0, channels, width):
        base = 2 * channels + at
        values[:, at : at + width] = dot(normed[...], qkv[:, base : base + width]).astype(bf16)

    pair = 2 * HD
    first = lax.broadcasted_iota(jnp.int32, (rows, pair), 1) < HD
    place_a = lax.broadcasted_iota(jnp.int32, (rows, 2 * rows), 0) % PLACES
    place_b = lax.broadcasted_iota(jnp.int32, (rows, 2 * rows), 1) % PLACES
    same_place = place_a == place_b
    ones_a = jnp.where(first, 1.0, 0.0).astype(bf16)
    ones_b = jnp.where(first, 0.0, 1.0).astype(bf16)
    ones = jnp.concatenate([ones_a, ones_b], 0)
    for block in range(blocks):
        here = slice(block * rows, (block + 1) * rows)
        for at in range(0, channels, pair):
            query = queries[here, at : at + pair]
            key = keys[here, at : at + pair]
            value = values[here, at : at + pair]
            both = jnp.concatenate([key * ones_a, key * ones_b], 0)
            scores = dot(query, both, ((1,), (1,))) * (1.0 / math.sqrt(HD))
            weights = jnp.where(same_place, jnp.exp(scores), 0.0).astype(bf16)
            both = jnp.concatenate([value * ones_a, value * ones_b], 0)
            summed = dot(weights, jnp.concatenate([both, ones], 1))
            mixed[here, at : at + pair] = (summed[:, :pair] / summed[:, pair:]).astype(bf16)

    attended = dot(mixed[...], outer[...]).astype(bf16).astype(jnp.float32)
    kept[...] = (kept[...].astype(jnp.float32) + attended).astype(bf16)
    chip = lax.axis_index("tm") // 2
    for k, piece in enumerate(pieces):
        for side in range(2):
            frame = 2 * jnp.bitwise_xor(chip, k) + side
            for block in range(blocks):
                at = pl.multiple_of(block * rows + frame * PLACES, PLACES)
                to = side * across + block * PLACES
                piece[to : to + PLACES, :] = kept[pl.ds(at, PLACES), :]


def fetch_kernel(count, *refs):
    arrived = refs[-1]
    copies = [
        pltpu.make_async_copy(refs[at], refs[count + at], arrived.at[at]) for at in range(count)
    ]
    for copy in copies:
        copy.start()
    for copy in copies:
        copy.wait()


def fetched(*parts):
    return pl.pallas_call(
        functools.partial(fetch_kernel, len(parts)),
        out_shape=[jax.ShapeDtypeStruct(part.shape, part.dtype) for part in parts],
        in_specs=[pl.BlockSpec(memory_space=pltpu.HBM)] * len(parts),
        out_specs=[VMEM] * len(parts),
        scratch_shapes=[pltpu.SemaphoreType.DMA((len(parts),))],
        compiler_params=pltpu.CompilerParams(vmem_limit_bytes=2**20),
        name="fetch",
    )(*(pltpu.with_memory_space_constraint(part, pltpu.HBM) for part in parts))


def time_mixing(received, conv_weight, qkv_weight, attn_out_weight):
    frames, across, channels = received.shape
    bf16 = jnp.bfloat16
    rows = pltpu.VMEM((frames * across, channels), bf16)
    far = pl.BlockSpec(memory_space=pltpu.HBM)
    return pl.pallas_call(
        mixing_kernel,
        out_shape=[jax.ShapeDtypeStruct((2 * across, channels), bf16)] * (frames // 2),
        in_specs=[VMEM] * 3 + [far],
        out_specs=[VMEM] * (frames // 2),
        scratch_shapes=[rows] * 6
        + [pltpu.VMEM(qkv_weight.shape, bf16), pltpu.SemaphoreType.DMA((3,))],
        compiler_params=pltpu.CompilerParams(vmem_limit_bytes=28 * 2**20),
        name="mixing",
    )(
        received,
        conv_weight,
        attn_out_weight,
        pltpu.with_memory_space_constraint(qkv_weight, pltpu.HBM),
    )


def dispatch_kernel(
    chips, classes, capacity, parts, own_ids, other_ids, router, *refs
):
    own, other, outs = refs[:parts], refs[parts : 2 * parts], refs[2 * parts :]
    boxes, combs = outs[:chips], outs[chips:]
    tokens = own_ids.shape[1]
    experts = router.shape[0]
    slots = chips * capacity
    at = lax.axis_index("tm")
    chip, core, mine = at // 2, at % 2, lax.axis_index("group") // 2
    slot = lax.broadcasted_iota(jnp.int32, (slots, tokens), 0)
    target = jnp.bitwise_xor(slot // capacity, chip)
    target = (2 * target + core) * classes + mine
    order = slot % capacity
    before = lax.broadcasted_iota(jnp.int32, (tokens, tokens), 0)
    after = lax.broadcasted_iota(jnp.int32, (tokens, tokens), 1)
    earlier = (before < after).astype(jnp.float32).astype(jnp.bfloat16)
    kinds = lax.broadcasted_iota(jnp.int32, (experts, tokens), 0)
    for side, (pieces, ids) in enumerate(((own, own_ids), (other, other_ids))):
        rows = jnp.concatenate([piece[...] for piece in pieces], 0)
        first, second = ids[0:1, :], ids[1:2, :]
        logits = dot(router[...], rows, ((1,), (1,)))
        gate_a = jax.nn.sigmoid(
            jnp.sum(jnp.where(kinds == first, logits, 0.0), 0, keepdims=True)
        )
        gate_b = jax.nn.sigmoid(
            jnp.sum(jnp.where(kinds == second, logits, 0.0), 0, keepdims=True)
        )
        whole = gate_a + gate_b
        hit_a, hit_b = target == first, target == second
        member = jnp.where(hit_a | hit_b, 1.0, 0.0)
        rank = dot(member.astype(jnp.bfloat16), earlier)
        taken = jnp.where(rank == order.astype(jnp.float32), member, 0.0)
        share = jnp.where(hit_a, gate_a / whole, gate_b / whole)
        combs[side][...] = (taken * share).astype(jnp.bfloat16)
        moved = dot(taken.astype(jnp.bfloat16), rows).astype(jnp.bfloat16)
        for k in range(chips):
            boxes[k][side * capacity : (side + 1) * capacity, :] = moved[
                k * capacity : (k + 1) * capacity, :
            ]


def dispatched(own, other, own_ids, other_ids, router, chips, classes, capacity):
    tokens, channels = own_ids.shape[1], own[0].shape[1]
    bf16 = jnp.bfloat16
    shapes = [jax.ShapeDtypeStruct((2 * capacity, channels), bf16)] * chips
    shapes += [jax.ShapeDtypeStruct((chips * capacity, tokens), bf16)] * 2
    outs = pl.pallas_call(
        functools.partial(dispatch_kernel, chips, classes, capacity, len(own)),
        out_shape=shapes,
        in_specs=[VMEM] * (3 + 2 * len(own)),
        out_specs=[VMEM] * (chips + 2),
        compiler_params=LIMIT,
        name="dispatch",
    )(own_ids, other_ids, router, *own, *other)
    return outs[:chips], outs[chips:]


def expert_kernel(chips, *refs):
    inputs, (inner, outer) = refs[:chips], refs[chips : chips + 2]
    outputs, (gathered, total) = refs[chips + 2 : -2], refs[-2:]
    size = inputs[0].shape[0]
    units = inner.shape[1]
    tile = units // 4
    for k in range(chips):
        gathered[k * size : (k + 1) * size, :] = inputs[k][...]
    for at in range(0, units, tile):
        hidden = jax.nn.gelu(dot(gathered[...], inner[:, at : at + tile])).astype(jnp.bfloat16)
        part = dot(hidden, outer[at : at + tile, :])
        if at == 0:
            total[...] = part
        elif at + tile < units:
            total[...] += part
        else:
            done = (total[...] + part).astype(jnp.bfloat16)
            step = outputs[0].shape[0]
            for k, out in enumerate(outputs):
                out[...] = done[k * step : (k + 1) * step, :]


def expert_rows(pieces, inner, outer, joined):
    chips = len(pieces)
    size, channels = pieces[0].shape
    units = inner.shape[1]
    rows = chips * size
    count = 1 if joined else chips
    return pl.pallas_call(
        functools.partial(expert_kernel, chips),
        out_shape=[jax.ShapeDtypeStruct((rows // count, channels), jnp.bfloat16)] * count,
        in_specs=[VMEM] * (chips + 2),
        out_specs=[VMEM] * count,
        scratch_shapes=[
            pltpu.VMEM((rows, channels), jnp.bfloat16),
            pltpu.VMEM((rows, channels), jnp.float32),
        ],
        compiler_params=pltpu.CompilerParams(vmem_limit_bytes=20 * 2**20),
        cost_estimate=pl.CostEstimate(
            flops=4 * rows * channels * units,
            transcendentals=rows * units,
            bytes_accessed=4 * channels * units,
        ),
        name="experts",
    )(*pieces, inner, outer)


def pair_kernel(first, one, two, *outs):
    size = outs[0].shape[0]
    for k, out in enumerate(outs):
        both = one[(first + k) * size : (first + k + 1) * size, :].astype(jnp.float32)
        both = both + two[k * size : (k + 1) * size, :].astype(jnp.float32)
        out[...] = both.astype(out.dtype)


def pair_summed(one, two, first, count):
    rows, channels = two.shape
    return pl.pallas_call(
        functools.partial(pair_kernel, first),
        out_shape=[jax.ShapeDtypeStruct((rows // count, channels), one.dtype)] * count,
        in_specs=[VMEM] * 2,
        out_specs=[VMEM] * count,
        compiler_params=LIMIT,
        name="pair",
    )(one, two)


def combine_kernel(chips, *refs):
    pieces, combs = refs[:chips], refs[chips : chips + 2]
    own, other = refs[chips + 2 :]
    capacity = pieces[0].shape[0] // 2
    for side, out in enumerate((own, other)):
        rows = jnp.concatenate(
            [pieces[k][side * capacity : (side + 1) * capacity, :] for k in range(chips)], 0
        )
        out[...] = dot(combs[side][...], rows, ((0,), (0,))).astype(out.dtype)


def combined(pieces, combs):
    chips = len(pieces)
    tokens = combs[0].shape[1]
    channels = pieces[0].shape[1]
    return pl.pallas_call(
        functools.partial(combine_kernel, chips),
        out_shape=[
            jax.ShapeDtypeStruct((tokens, channels), jnp.float32),
            jax.ShapeDtypeStruct((tokens, channels), jnp.bfloat16),
        ],
        in_specs=[VMEM] * (chips + 2),
        out_specs=[VMEM] * 2,
        compiler_params=LIMIT,
        name="combine",
    )(*pieces, *combs)


def norm_kernel(chips, *refs):
    sides, (stream, own, other) = (refs[:chips], refs[chips : 2 * chips]), refs[2 * chips :]
    at = lax.axis_index("tm")
    chip, core = at // 2, at % 2
    across = refs[0].shape[0] // 2
    for k in range(chips):
        for far, pieces in enumerate(sides):
            block = 2 * jnp.bitwise_xor(chip, k) + (1 - core if far else core)
            to = pl.ds(pl.multiple_of(block * across, across), across)
            rows = pieces[k][pl.ds(pl.multiple_of(core * across, across), across), :]
            stream[to, :] = rows
            own[to, :] = layer_normed(rows)
            rows = pieces[k][pl.ds(pl.multiple_of((1 - core) * across, across), across), :]
            other[to, :] = layer_normed(rows)


def rows_normed(mine, theirs):
    chips = len(mine)
    size, channels = mine[0].shape
    return pl.pallas_call(
        functools.partial(norm_kernel, chips),
        out_shape=[jax.ShapeDtypeStruct((chips * size, channels), mine[0].dtype)] * 3,
        in_specs=[VMEM] * (2 * chips),
        out_specs=[VMEM] * 3,
        compiler_params=LIMIT,
        name="norm",
    )(*mine, *theirs)


def sum_kernel(halves, *refs):
    whole, (first, second), out = refs[:-1], halves, refs[-1]
    parts, whole = whole[-(first + second) :], whole[: -(first + second)]
    at = 0
    for group in (parts[:first], parts[first:]):
        here = slice(at, at + group[0].shape[0])
        total = whole[0][here, :].astype(jnp.float32)
        for part in whole[1:]:
            total = total + part[here, :].astype(jnp.float32)
        for part in group:
            total = total + part[...].astype(jnp.float32)
        out[here, :] = total.astype(out.dtype)
        at = here.stop


def summed(whole, first, second):
    rows = [*whole, *first, *second]
    return pl.pallas_call(
        functools.partial(sum_kernel, (len(first), len(second))),
        out_shape=jax.ShapeDtypeStruct(whole[0].shape, whole[0].dtype),
        in_specs=[VMEM] * len(rows),
        out_specs=VMEM,
        compiler_params=LIMIT,
        name="total",
    )(*rows)


def body(
    tokens,
    conv_weight,
    qkv_weight,
    attn_out_weight,
    router_weight,
    expert_ids,
    expert_in,
    expert_out,
):
    shards = lax.axis_size("tm")
    groups = lax.axis_size("group")
    chips = shards // 2
    classes = groups // 2
    spatial, channels = tokens.shape[1:]
    across = spatial // shards
    experts = router_weight.shape[1]
    capacity = 4 * spatial // experts

    def swapped(rows, axis, step):
        if step == 0:
            return rows
        size = lax.axis_size(axis)
        return lax.ppermute(rows, axis, [(i, i ^ step) for i in range(size)])

    routed = expert_ids.reshape(spatial, 2).T
    pair = jnp.concatenate([routed, swapped(routed, "tm", 1)], 0)
    blocked = [step for step in range(groups) if step != 1]
    ids = {step: swapped(pair, "group", step) for step in blocked}

    received = lax.all_to_all(
        tokens.reshape(1, shards, across, channels),
        "tm",
        split_axis=1,
        concat_axis=0,
        tiled=True,
    ).reshape(shards, across, channels)
    conv_weight, attn_out_weight = fetched(conv_weight, attn_out_weight)
    pieces = time_mixing(received, conv_weight, qkv_weight, attn_out_weight)
    inner, outer = fetched(expert_in[0], expert_out[0])
    mine = [swapped(pieces[k], "tm", 2 * k) for k in range(chips)]
    theirs = [swapped(mine[k], "tm", 1) for k in range(chips)]
    stream, normed, beside = rows_normed(mine, theirs)

    router = router_weight.T
    blocks = {0: (normed,)}
    for step in blocked[1:]:
        sources = blocks[step - 1] if step % 2 else blocks[0]
        blocks[step] = tuple(swapped(rows, "group", 1 if step % 2 else step) for rows in sources)
    whole, first, second, waiting = [stream], [], [], None
    cut = spatial * 5 // 8
    bf16 = jnp.bfloat16
    for step in blocked:
        own = blocks[step]
        other = tuple(swapped(rows, "tm", 1) for rows in own)
        other = other if step else (beside,)
        boxes, combs = dispatched(
            own,
            other,
            ids[step][:2],
            ids[step][2:],
            router,
            chips,
            classes,
            capacity,
        )
        pieces = [swapped(boxes[k], "tm", 2 * k) for k in range(chips)]
        results = expert_rows(pieces, inner, outer, step == 0)
        if step == 0:
            near = [swapped(pieces[k], "group", 1) for k in range(chips)]
            joined, results = results[0], []
            for at in (0, chips // 2):
                others = expert_rows(near[at : at + chips // 2], inner, outer, True)
                others = swapped(others[0], "group", 1)
                results += pair_summed(joined, others, at, chips // 2)
        returned = [swapped(results[k], "tm", 2 * k) for k in range(chips)]
        here, there = combined(returned, combs)
        across_core = swapped(there, "tm", 1)
        if step == 0:
            whole += [here, across_core]
            continue
        mixed = here + across_core.astype(jnp.float32)
        first.append(swapped(mixed[:cut].astype(bf16), "group", step))
        if step % 2 == 0:
            waiting = mixed[cut:]
        else:
            near = swapped(mixed[cut:].astype(bf16), "group", 1)
            joint = (waiting + near.astype(jnp.float32)).astype(bf16)
            second.append(swapped(joint, "group", step - 1))
    return summed(whole, first, second).reshape(1, spatial, channels)


def solution(mesh):
    placed = (
        P("tm", "group", None),
        P(),
        P(),
        P(),
        P(),
        P("tm", "group", None),
        P(("tm", "group"), None, None),
        P(("tm", "group"), None, None),
    )
    return jax.shard_map(
        body, mesh=mesh, in_specs=placed, out_specs=P("tm", "group", None), check_vma=False
    )
```
